32 devices in a mesh: row: 4 (over y, x), col: 4 (over z), layer: 2 (over core).
Axes of the slice: x: 2, y: 2, z: 4, core: 2. Of those that a mesh axis runs over, the one named last changes fastest.
Arguments:
- occupancy: int32 [4, 512], P(None, ('col', 'layer')), may hold values from 0 to 1, as said below
- tiles: bfloat16 [8, 4, 64, 256, 256], P(('col', 'layer'), 'row'), may hold values from -0.0234375 to 0.0234375
- panel: float32 [131072, 2048], P(('col', 'layer'), 'row'), may hold values from -6 to 6
Outputs:
- product: float32 [1024, 2048], P(('col', 'layer'), 'row')
The draws below stay inside these ranges and needn't reach their ends.
Inputs may be any that keep to these rules, and one draw needn't show every extreme that they name: `occupancy`: in every draw one whole column block is occupied, so that the stored tiles of one device fill all 64 slots.
All inputs are finite; a program needn't handle non-finite values.
Results may differ from the reference program's by a relative error of at most 0.0029.
Values may be sent and summed in bfloat16 or wider, within the bound.
No kernel may reach another device: no remote copies, remote signals or barrier semaphores. Data moves between devices by JAX's collectives and lax.ppermute only.
A program may use at most 192 MiB of HBM per device.

```python
import jax
import jax.numpy as jnp
from jax import lax

TILE = 256
K = 131072
N = 2048
MT = 4
NKB = 8
SLOTS = 64
N_ROW = 4
N_COL = 4
N_LAYER = 2


def draw_occupancy(key, part):
    key_rows, key_cols, key_coin, key_block = jax.random.split(jax.random.fold_in(key, 7), 4)
    tile_cols = K // TILE
    row_power = jax.random.randint(key_rows, (MT,), 0, 4)
    col_power = jax.random.randint(key_cols, (tile_cols,), 1, 5)
    weight = jnp.left_shift(jnp.int32(1), row_power)[:, None] * jnp.left_shift(jnp.int32(1), col_power)[None, :]
    coin = jax.random.randint(key_coin, (MT, tile_cols), 0, 64)
    occupied = (coin < weight).astype(jnp.int32)
    blocks = N_COL * N_LAYER
    width = tile_cols // blocks
    chosen = jax.random.randint(key_block, (), 0, blocks)
    block_of = jnp.arange(tile_cols, dtype=jnp.int32) // width
    return jnp.where(block_of[None, :] == chosen, 1, occupied).astype(jnp.int32)


def levels(own_key, extent, cuts, low, high):
    gain = 1.0
    for position, shards_of in cuts:
        steps = jax.random.uniform(jax.random.fold_in(jax.random.fold_in(own_key, 6), position), (shards_of,), jnp.float32, low / len(cuts), high / len(cuts))
        gain = gain * jnp.repeat(jnp.exp(steps), extent[position] // shards_of).reshape((-1,) + (1,) * (len(extent) - 1 - position))
    return gain


def gaussian(key, dims, scale, most, cuts=(), held_as=jnp.bfloat16):
    array = jax.random.normal(key, dims, jnp.float32) * scale
    if len(cuts) > 0:
        array = levels(key, dims, cuts, -0.22, 0.18) * array
    return jnp.clip(array, min=-most, max=most).astype(held_as)


def setup_inputs(seed: int = 0) -> dict:
    key_list = jax.random.split(jax.random.key(seed), 4)
    occupancy = draw_occupancy(jax.random.fold_in(key_list[3], 71), 0)
    tiles = gaussian(key_list[1], (NKB, N_ROW, SLOTS, TILE, TILE), (K // 2) ** -0.5, 0.0234375, ((0, 8), (1, 4)))
    panel = gaussian(key_list[2], (K, N), 1.0, 6.0, ((0, 8), (1, 4)), jnp.float32)
    return dict(occupancy=occupancy, tiles=tiles, panel=panel)


def positions(occ_block):
    flat = occ_block.reshape(-1).astype(jnp.int32)
    count = flat.shape[0]
    rank = jnp.cumsum(flat).astype(jnp.int32) - 1
    index = jnp.arange(count, dtype=jnp.int32)
    match = (flat[None, :] == 1) & (rank[None, :] == index[:, None])
    where_at = jnp.sum(jnp.where(match, index[None, :], 0), axis=1).astype(jnp.int32)
    valid = jnp.sum(match.astype(jnp.int32), axis=1).astype(jnp.int32)
    width = occ_block.shape[1]
    return where_at // width, where_at % width, valid


def reference(occupancy, tiles, panel):
    ktb = K // (N_COL * N_LAYER * TILE)
    nkb = N_COL * N_LAYER
    panel_low = panel.astype(jnp.bfloat16).reshape(nkb, ktb, TILE, N)
    occ_blocks = jnp.transpose(occupancy.reshape(MT, nkb, ktb), (1, 0, 2))
    packed = tiles.reshape(nkb, -1, TILE, TILE)

    def step(total, block):
        occ_block, tile_block, panel_block = block
        rows_at, cols_at, valid = positions(occ_block)
        rhs = panel_block[cols_at]
        prod = jnp.einsum('jab,jbn->jan', tile_block.astype(jnp.float32), rhs.astype(jnp.float32),
                          precision=lax.Precision.HIGHEST)
        weights = ((rows_at[None, :] == jnp.arange(MT, dtype=jnp.int32)[:, None]) & (valid[None, :] == 1)).astype(jnp.float32)
        add = jnp.einsum('tj,jan->tan', weights, prod, precision=lax.Precision.HIGHEST)
        return total + add, None

    start = jnp.zeros((MT, TILE, N), jnp.float32)
    total, _ = lax.scan(step, start, (occ_blocks, packed, panel_low))
    return total.reshape(MT * TILE, N)
```

```python
import functools

import jax
import jax.numpy as jnp
from jax import lax
from jax.experimental import pallas as pl
from jax.experimental.pallas import tpu as pltpu
from jax.sharding import PartitionSpec as P

LATENCY = 2
ANY = pl.BlockSpec(memory_space=pl.ANY)
SMEM = pl.BlockSpec(memory_space=pltpu.SMEM)


def ring_order(n_row):
    side = int(round(n_row ** 0.5))
    if side * side != n_row or side % 2:
        return list(range(n_row))
    path = [(0, x) for x in range(side)]
    for x in reversed(range(side)):
        ys = range(1, side) if (side - 1 - x) % 2 == 0 else reversed(range(1, side))
        path += [(y, x) for y in ys]
    return [y * side + x for y, x in path]


def plan_kernel(order, slots, chunk, steps, me_ref, occ_ref, where_ref, sched_ref, meta_ref, start_ref, quota_ref, owner_ref, held_ref):
    tile_rows, width = occ_ref.shape
    n = len(order)
    pair = 2 * chunk

    def mark(e, rank):
        where_ref[rank] = e
        return rank + occ_ref[e // width, e % width]

    count = lax.fori_loop(0, tile_rows * width, mark, jnp.int32(0))
    for p in range(n):
        stored = jnp.clip(count - slots * order[p], 0, slots)
        owner_ref[p] = order[p]
        held_ref[p] = stored
        quota_ref[p] = (stored + pair - 1) // pair

    def clear(t, carry):
        for f in range(8):
            sched_ref[t, f] = 0
        return carry

    lax.fori_loop(0, steps, clear, 0)
    total = jnp.int32(0)
    me = me_ref[0]
    for d in range(2):
        back = n - 1 if d == 0 else 1

        def first(p, carry):
            start_ref[0, p] = 0
            return jnp.maximum(carry, quota_ref[p])

        total = lax.fori_loop(0, n, first, total)

        def hop(h, carry):
            def place(p, c):
                up = (p + back) % n
                source = (p + h * back) % n
                last = (p + (h - 1) * back) % n
                begin = jnp.maximum(start_ref[h - 1, p] + quota_ref[last], start_ref[h - 1, up] + LATENCY)
                start_ref[h, p] = begin
                amount = quota_ref[source]
                return jnp.where(amount > 0, jnp.maximum(c, begin + amount), c)

            return lax.fori_loop(0, n, place, carry)

        total = lax.fori_loop(1, n - 1, hop, total)

        def fill(h, carry):
            up = (me + back) % n
            source = (me + h * back) % n
            begin = start_ref[h, me]
            arrived = start_ref[jnp.maximum(h - 1, 0), up]

            def send(q, c):
                sched_ref[begin + q, d] = jnp.where(h == 0, 2 * q + d, -1 - (arrived + q))
                return c

            lax.fori_loop(0, quota_ref[source], send, 0)
            origin = (up + h * back) % n
            begin_up = start_ref[h, up]

            def receive(q, c):
                slot = (2 * q + d) * chunk
                sched_ref[begin_up + q, 2 + 2 * d] = owner_ref[origin] * slots + slot
                sched_ref[begin_up + q, 3 + 2 * d] = jnp.clip(held_ref[origin] - slot, 0, chunk)
                return c

            lax.fori_loop(0, quota_ref[origin], receive, 0)
            return carry

        lax.fori_loop(0, n - 1, fill, 0)
    meta_ref[0] = total
    meta_ref[1] = held_ref[me]
    meta_ref[2] = owner_ref[me] * slots


def plan(occupancy, order, slots, chunk, steps):
    n = len(order)
    place = [0] * n
    for p, r in enumerate(order):
        place[r] = p
    me = jnp.asarray(place, jnp.int32)[lax.axis_index("row")].reshape(1)
    size = occupancy.shape[0] * occupancy.shape[1]
    return pl.pallas_call(
        functools.partial(plan_kernel, order, slots, chunk, steps),
        out_shape=(
            jax.ShapeDtypeStruct((size,), jnp.int32),
            jax.ShapeDtypeStruct((steps, 8), jnp.int32),
            jax.ShapeDtypeStruct((4,), jnp.int32),
        ),
        in_specs=[SMEM, SMEM],
        out_specs=(SMEM, SMEM, SMEM),
        scratch_shapes=[
            pltpu.SMEM((n, n), jnp.int32),
            pltpu.SMEM((n,), jnp.int32),
            pltpu.SMEM((n,), jnp.int32),
            pltpu.SMEM((n,), jnp.int32),
        ],
        name="plan",
    )(me, occupancy)


def accumulate(acc_ref, code, width, tile, panel_block):
    side = tile.shape[0]
    row = pl.multiple_of((code // width) * side, side)
    acc_ref[pl.ds(row, side), :] += jnp.dot(
        tile, panel_block.astype(jnp.bfloat16), preferred_element_type=jnp.float32
    )


def own_kernel(depth, where_ref, meta_ref, tiles_ref, panel_ref, acc_ref, tbuf, pbuf, tsem, psem):
    width = panel_ref.shape[0]
    held, base = meta_ref[1], meta_ref[2]
    acc_ref[...] = jnp.zeros_like(acc_ref)

    def copies(e):
        s = e % depth
        code = where_ref[base + e]
        return (
            pltpu.make_async_copy(tiles_ref.at[e], tbuf.at[s], tsem.at[s]),
            pltpu.make_async_copy(panel_ref.at[code % width], pbuf.at[s], psem.at[s]),
        )

    def begin(e):
        for c in copies(e):
            c.start()

    def warm(e, carry):
        begin(e)
        return carry

    lax.fori_loop(0, jnp.minimum(held, depth - 1), warm, 0)

    def body(e, carry):
        @pl.when(e + depth - 1 < held)
        def _():
            begin(e + depth - 1)

        for c in copies(e):
            c.wait()
        s = e % depth
        accumulate(acc_ref, where_ref[base + e], width, tbuf[s], pbuf[s])
        return carry

    lax.fori_loop(0, held, body, 0)


def own_product(where, meta, tiles, panel, tile_rows):
    slots, side, _ = tiles.shape
    columns = panel.shape[2]
    depth = 8
    return pl.pallas_call(
        functools.partial(own_kernel, depth),
        out_shape=jax.ShapeDtypeStruct((tile_rows * side, columns), jnp.float32),
        in_specs=[SMEM, SMEM, ANY, ANY],
        out_specs=pl.BlockSpec((tile_rows * side, columns), lambda: (0, 0)),
        scratch_shapes=[
            pltpu.VMEM((depth, side, side), jnp.bfloat16),
            pltpu.VMEM((depth, side, columns), jnp.float32),
            pltpu.SemaphoreType.DMA((depth,)),
            pltpu.SemaphoreType.DMA((depth,)),
        ],
        compiler_params=pltpu.CompilerParams(vmem_limit_bytes=32 << 20),
        cost_estimate=pl.CostEstimate(flops=2 * slots * side * side * columns, bytes_accessed=slots * side * (2 * side + 4 * columns), transcendentals=0),
        name="own",
    )(where, meta, tiles, panel)


def step_kernel(chunk, relay, where_ref, sched_ref, t_ref, ra_ref, rb_ref, tiles_ref, panel_ref, acc_in, log_in, acc_ref, *rest):
    if relay:
        log_ref, sa_ref, sb_ref, rbuf, pbuf, rsem, psem, lsem, ssem = rest
    else:
        rbuf, pbuf, rsem, psem = rest
    width = panel_ref.shape[0]
    t = t_ref[0]
    got = (ra_ref, rb_ref)
    base = [sched_ref[t - 1, 2 + 2 * d] for d in range(2)]
    count = [sched_ref[t - 1, 3 + 2 * d] for d in range(2)]
    fetch = [pltpu.make_async_copy(got[d], rbuf.at[d], rsem.at[d]) for d in range(2)]
    for d in range(2):
        fetch[d].start()

    def panel_copy(d, e):
        code = where_ref[base[d] + e]
        return pltpu.make_async_copy(panel_ref.at[code % width], pbuf.at[d, e], psem.at[d, e])

    for d in range(2):
        def begin(e, carry):
            panel_copy(d, e).start()
            return carry

        lax.fori_loop(0, count[d], begin, 0)
    if relay:
        out = (sa_ref, sb_ref)
        for d in range(2):
            item = sched_ref[t + 1, d]
            logged = -1 - item

            @pl.when(item >= 0)
            def _():
                first = pl.multiple_of(item * chunk, chunk)
                pltpu.make_async_copy(tiles_ref.at[pl.ds(first, chunk)], out[d], ssem.at[d]).start()

            @pl.when((item < 0) & (logged == t - 1))
            def _():
                pltpu.make_async_copy(got[d], out[d], ssem.at[d]).start()

            @pl.when((item < 0) & (logged != t - 1))
            def _():
                pltpu.make_async_copy(log_in.at[d, logged], out[d], ssem.at[d]).start()

    for d in range(2):
        fetch[d].wait()
        if relay:
            pltpu.make_async_copy(rbuf.at[d], log_ref.at[d, t - 1], lsem.at[d]).start()
    acc_ref[...] = acc_in[...]
    for d in range(2):
        def body(e, carry):
            panel_copy(d, e).wait()
            accumulate(acc_ref, where_ref[base[d] + e], width, rbuf[d, e], pbuf[d, e])
            return carry

        lax.fori_loop(0, count[d], body, 0)
    if relay:
        for d in range(2):
            pltpu.make_async_copy(rbuf.at[d], log_ref.at[d, t - 1], lsem.at[d]).wait()
            pltpu.make_async_copy(tiles_ref.at[pl.ds(0, chunk)], out[d], ssem.at[d]).wait()


def step(where, sched, t, ra, rb, tiles, panel, acc, log, relay=True):
    chunk, side, _ = ra.shape
    columns = panel.shape[2]
    acc_spec = pl.BlockSpec(acc.shape, lambda: (0, 0))
    send = jax.ShapeDtypeStruct(ra.shape, ra.dtype)
    send_spec = pl.BlockSpec(ra.shape, lambda: (0, 0, 0))
    out_shape = [jax.ShapeDtypeStruct(acc.shape, acc.dtype)]
    out_specs = [acc_spec]
    scratch = [
        pltpu.VMEM((2,) + ra.shape, ra.dtype),
        pltpu.VMEM((2, chunk, side, columns), jnp.float32),
        pltpu.SemaphoreType.DMA((2,)),
        pltpu.SemaphoreType.DMA((2, chunk)),
    ]
    aliases = {7: 0}
    if relay:
        out_shape += [jax.ShapeDtypeStruct(log.shape, log.dtype), send, send]
        out_specs += [ANY, send_spec, send_spec]
        scratch += [pltpu.SemaphoreType.DMA((2,)), pltpu.SemaphoreType.DMA((2,))]
        aliases[8] = 1
    return pl.pallas_call(
        functools.partial(step_kernel, chunk, relay),
        out_shape=out_shape,
        in_specs=[SMEM, SMEM, SMEM, ANY, ANY, ANY, ANY, acc_spec, ANY],
        out_specs=out_specs,
        scratch_shapes=scratch,
        input_output_aliases=aliases,
        compiler_params=pltpu.CompilerParams(vmem_limit_bytes=48 << 20),
        cost_estimate=pl.CostEstimate(flops=4 * chunk * side * side * columns, bytes_accessed=2 * chunk * side * (4 * side + 4 * columns), transcendentals=0),
        name="step" if relay else "last",
    )(where, sched, t.reshape(1), ra, rb, tiles, panel, acc, log)


def blank(shape, dtype):
    return pl.pallas_call(lambda out: None, out_shape=jax.ShapeDtypeStruct(shape, dtype), out_specs=ANY, name="blank")()


def scatter_sum(total, n_col, n_layer):
    columns = total.shape[1]
    parts = total.reshape(n_col, n_layer, -1, columns)
    mine = lax.axis_index("layer")
    kept = lax.dynamic_index_in_dim(parts, mine, 1, keepdims=False)
    for k in range(1, n_layer):
        away = lax.dynamic_index_in_dim(parts, (mine + k) % n_layer, 1, keepdims=False)
        kept = kept + lax.ppermute(away, "layer", [(i, (i + k) % n_layer) for i in range(n_layer)])
    mine = lax.axis_index("col")
    result = lax.dynamic_index_in_dim(kept, mine, 0, keepdims=False)
    for k in range(1, n_col):
        away = lax.dynamic_index_in_dim(kept, (mine + k) % n_col, 0, keepdims=False)
        result = result + lax.ppermute(away, "col", [(i, (i + k) % n_col) for i in range(n_col)])
    return result


def local(n_row, n_col, n_layer, occupancy, tiles, panel):
    tile_rows, width = occupancy.shape
    slots, side = tiles.shape[2], tiles.shape[3]
    tiles = tiles.reshape(slots, side, side)
    panel = panel.reshape(width, side, -1)
    chunk = max(1, slots // 8)
    most = -(-slots // (2 * chunk))
    steps = (n_row - 2) * max(most, LATENCY) + most + 4
    order = ring_order(n_row)
    up = [(order[p], order[(p + 1) % n_row]) for p in range(n_row)]
    down = [(b, a) for a, b in up]
    first = [tiles[k * chunk:(k + 1) * chunk] for k in range(4) if (k + 1) * chunk <= slots]
    first = first + first[: 4 - len(first)]
    ra = lax.ppermute(first[0], "row", up)
    rb = lax.ppermute(first[1], "row", down)
    where, sched, meta = plan(occupancy, order, slots, chunk, steps)
    acc = own_product(where, meta, tiles, panel, tile_rows)
    log = blank((2, steps, chunk, side, side), tiles.dtype)

    def advance(t, sa, sb, ra, rb, acc, log):
        na = lax.ppermute(sa, "row", up)
        nb = lax.ppermute(sb, "row", down)
        acc, log, sa, sb = step(where, sched, t, ra, rb, tiles, panel, acc, log)
        return sa, sb, na, nb, acc, log

    state = advance(jnp.int32(1), first[2], first[3], ra, rb, acc, log)

    def body(carry):
        t, state = carry
        for u in range(2):
            state = advance(t + u, *state)
        return t + 2, state

    t, (_, _, ra, rb, acc, log) = lax.while_loop(lambda c: c[0] < meta[0], body, (jnp.int32(2), state))
    (acc,) = step(where, sched, t, ra, rb, tiles, panel, acc, log, relay=False)
    return scatter_sum(acc, n_col, n_layer)


def solution(mesh):
    placed = (
        P(None, ("col", "layer")),
        P(("col", "layer"), "row", None, None, None),
        P(("col", "layer"), "row"),
    )
    sizes = tuple(mesh.shape[name] for name in ("row", "col", "layer"))
    return jax.shard_map(
        functools.partial(local, *sizes), mesh=mesh, in_specs=placed, out_specs=P(("col", "layer"), "row"), check_vma=False
    )
```

```python
import functools

import jax
import jax.numpy as jnp
from jax import lax
from jax.experimental import pallas as pl
from jax.experimental.pallas import tpu as pltpu
from jax.sharding import PartitionSpec as P

LATENCY = 2
ANY = pl.BlockSpec(memory_space=pl.ANY)
SMEM = pl.BlockSpec(memory_space=pltpu.SMEM)


def ring_order(n_row):
    side = int(round(n_row ** 0.5))
    if side * side != n_row or side % 2:
        return list(range(n_row))
    path = [(0, x) for x in range(side)]
    for x in reversed(range(side)):
        ys = range(1, side) if (side - 1 - x) % 2 == 0 else reversed(range(1, side))
        path += [(y, x) for y in ys]
    return [y * side + x for y, x in path]


def plan_kernel(order, slots, chunk, steps, me_ref, occ_ref, where_ref, sched_ref, meta_ref, start_ref, quota_ref, owner_ref, held_ref):
    tile_rows, width = occ_ref.shape
    n = len(order)
    pair = 2 * chunk

    def mark(e, rank):
        where_ref[rank] = e
        return rank + occ_ref[e // width, e % width]

    count = lax.fori_loop(0, tile_rows * width, mark, jnp.int32(0))
    for p in range(n):
        stored = jnp.clip(count - slots * order[p], 0, slots)
        owner_ref[p] = order[p]
        held_ref[p] = stored
        quota_ref[p] = (stored + pair - 1) // pair

    def clear(t, carry):
        for f in range(8):
            sched_ref[t, f] = 0
        return carry

    lax.fori_loop(0, steps, clear, 0)
    total = jnp.int32(0)
    me = me_ref[0]
    for d in range(2):
        back = n - 1 if d == 0 else 1

        def first(p, carry):
            start_ref[0, p] = 0
            return jnp.maximum(carry, quota_ref[p])

        total = lax.fori_loop(0, n, first, total)

        def hop(h, carry):
            def place(p, c):
                up = (p + back) % n
                source = (p + h * back) % n
                last = (p + (h - 1) * back) % n
                begin = jnp.maximum(start_ref[h - 1, p] + quota_ref[last], start_ref[h - 1, up] + LATENCY)
                start_ref[h, p] = begin
                amount = quota_ref[source]
                return jnp.where(amount > 0, jnp.maximum(c, begin + amount), c)

            return lax.fori_loop(0, n, place, carry)

        total = lax.fori_loop(1, n - 1, hop, total)

        def fill(h, carry):
            up = (me + back) % n
            source = (me + h * back) % n
            begin = start_ref[h, me]
            arrived = start_ref[jnp.maximum(h - 1, 0), up]

            def send(q, c):
                sched_ref[begin + q, d] = jnp.where(h == 0, 2 * q + d, -1 - (arrived + q))
                return c

            lax.fori_loop(0, quota_ref[source], send, 0)
            origin = (up + h * back) % n
            begin_up = start_ref[h, up]

            def receive(q, c):
                slot = (2 * q + d) * chunk
                sched_ref[begin_up + q, 2 + 2 * d] = owner_ref[origin] * slots + slot
                sched_ref[begin_up + q, 3 + 2 * d] = jnp.clip(held_ref[origin] - slot, 0, chunk)
                return c

            lax.fori_loop(0, quota_ref[origin], receive, 0)
            return carry

        lax.fori_loop(0, n - 1, fill, 0)
    meta_ref[0] = total
    meta_ref[1] = held_ref[me]
    meta_ref[2] = owner_ref[me] * slots


def plan(occupancy, order, slots, chunk, steps):
    n = len(order)
    place = [0] * n
    for p, r in enumerate(order):
        place[r] = p
    me = jnp.asarray(place, jnp.int32)[lax.axis_index("row")].reshape(1)
    size = occupancy.shape[0] * occupancy.shape[1]
    return pl.pallas_call(
        functools.partial(plan_kernel, order, slots, chunk, steps),
        out_shape=(
            jax.ShapeDtypeStruct((size,), jnp.int32),
            jax.ShapeDtypeStruct((steps, 8), jnp.int32),
            jax.ShapeDtypeStruct((4,), jnp.int32),
        ),
        in_specs=[SMEM, SMEM],
        out_specs=(SMEM, SMEM, SMEM),
        scratch_shapes=[
            pltpu.SMEM((n, n), jnp.int32),
            pltpu.SMEM((n,), jnp.int32),
            pltpu.SMEM((n,), jnp.int32),
            pltpu.SMEM((n,), jnp.int32),
        ],
        name="plan",
    )(me, occupancy)


def accumulate(acc_ref, code, width, tile, panel_block):
    side = tile.shape[0]
    row = pl.multiple_of((code // width) * side, side)
    acc_ref[pl.ds(row, side), :] += jnp.dot(
        tile, panel_block.astype(jnp.bfloat16), preferred_element_type=jnp.float32
    )


def own_kernel(depth, where_ref, meta_ref, tiles_ref, panel_ref, acc_ref, tbuf, pbuf, tsem, psem):
    width = panel_ref.shape[0]
    held, base = meta_ref[1], meta_ref[2]
    acc_ref[...] = jnp.zeros_like(acc_ref)

    def copies(e):
        s = e % depth
        code = where_ref[base + e]
        return (
            pltpu.make_async_copy(tiles_ref.at[e], tbuf.at[s], tsem.at[s]),
            pltpu.make_async_copy(panel_ref.at[code % width], pbuf.at[s], psem.at[s]),
        )

    def begin(e):
        for c in copies(e):
            c.start()

    def warm(e, carry):
        begin(e)
        return carry

    lax.fori_loop(0, jnp.minimum(held, depth - 1), warm, 0)

    def body(e, carry):
        @pl.when(e + depth - 1 < held)
        def _():
            begin(e + depth - 1)

        for c in copies(e):
            c.wait()
        s = e % depth
        accumulate(acc_ref, where_ref[base + e], width, tbuf[s], pbuf[s])
        return carry

    lax.fori_loop(0, held, body, 0)


def own_product(where, meta, tiles, panel, tile_rows):
    slots, side, _ = tiles.shape
    columns = panel.shape[2]
    depth = 8
    return pl.pallas_call(
        functools.partial(own_kernel, depth),
        out_shape=jax.ShapeDtypeStruct((tile_rows * side, columns), jnp.float32),
        in_specs=[SMEM, SMEM, ANY, ANY],
        out_specs=pl.BlockSpec((tile_rows * side, columns), lambda: (0, 0)),
        scratch_shapes=[
            pltpu.VMEM((depth, side, side), jnp.bfloat16),
            pltpu.VMEM((depth, side, columns), jnp.float32),
            pltpu.SemaphoreType.DMA((depth,)),
            pltpu.SemaphoreType.DMA((depth,)),
        ],
        compiler_params=pltpu.CompilerParams(vmem_limit_bytes=32 << 20),
        cost_estimate=pl.CostEstimate(flops=2 * slots * side * side * columns, bytes_accessed=slots * side * (2 * side + 4 * columns), transcendentals=0),
        name="own",
    )(where, meta, tiles, panel)


def step_kernel(chunk, relay, where_ref, sched_ref, t_ref, ra_ref, rb_ref, tiles_ref, panel_ref, acc_in, log_in, acc_ref, *rest):
    if relay:
        log_ref, sa_ref, sb_ref, rbuf, pbuf, rsem, psem, lsem, ssem = rest
    else:
        rbuf, pbuf, rsem, psem = rest
    width = panel_ref.shape[0]
    t = t_ref[0]
    got = (ra_ref, rb_ref)
    base = [sched_ref[t - 1, 2 + 2 * d] for d in range(2)]
    count = [sched_ref[t - 1, 3 + 2 * d] for d in range(2)]
    fetch = [pltpu.make_async_copy(got[d], rbuf.at[d], rsem.at[d]) for d in range(2)]
    for d in range(2):
        fetch[d].start()

    def panel_copy(d, e):
        code = where_ref[base[d] + e]
        return pltpu.make_async_copy(panel_ref.at[code % width], pbuf.at[d, e], psem.at[d, e])

    for d in range(2):
        def begin(e, carry):
            panel_copy(d, e).start()
            return carry

        lax.fori_loop(0, count[d], begin, 0)
    if relay:
        out = (sa_ref, sb_ref)
        for d in range(2):
            item = sched_ref[t + 1, d]
            logged = -1 - item

            @pl.when(item >= 0)
            def _():
                first = pl.multiple_of(item * chunk, chunk)
                pltpu.make_async_copy(tiles_ref.at[pl.ds(first, chunk)], out[d], ssem.at[d]).start()

            @pl.when((item < 0) & (logged == t - 1))
            def _():
                pltpu.make_async_copy(got[d], out[d], ssem.at[d]).start()

            @pl.when((item < 0) & (logged != t - 1))
            def _():
                pltpu.make_async_copy(log_in.at[d, logged], out[d], ssem.at[d]).start()

    for d in range(2):
        fetch[d].wait()
        if relay:
            pltpu.make_async_copy(rbuf.at[d], log_ref.at[d, t - 1], lsem.at[d]).start()
    acc_ref[...] = acc_in[...]
    for d in range(2):
        def body(e, carry):
            panel_copy(d, e).wait()
            accumulate(acc_ref, where_ref[base[d] + e], width, rbuf[d, e], pbuf[d, e])
            return carry

        lax.fori_loop(0, count[d], body, 0)
    if relay:
        for d in range(2):
            pltpu.make_async_copy(rbuf.at[d], log_ref.at[d, t - 1], lsem.at[d]).wait()
            pltpu.make_async_copy(tiles_ref.at[pl.ds(0, chunk)], out[d], ssem.at[d]).wait()


def step(where, sched, t, ra, rb, tiles, panel, acc, log, relay=True):
    chunk, side, _ = ra.shape
    columns = panel.shape[2]
    acc_spec = pl.BlockSpec(acc.shape, lambda: (0, 0))
    send = jax.ShapeDtypeStruct(ra.shape, ra.dtype)
    send_spec = pl.BlockSpec(ra.shape, lambda: (0, 0, 0))
    out_shape = [jax.ShapeDtypeStruct(acc.shape, acc.dtype)]
    out_specs = [acc_spec]
    scratch = [
        pltpu.VMEM((2,) + ra.shape, ra.dtype),
        pltpu.VMEM((2, chunk, side, columns), jnp.float32),
        pltpu.SemaphoreType.DMA((2,)),
        pltpu.SemaphoreType.DMA((2, chunk)),
    ]
    aliases = {7: 0}
    if relay:
        out_shape += [jax.ShapeDtypeStruct(log.shape, log.dtype), send, send]
        out_specs += [ANY, send_spec, send_spec]
        scratch += [pltpu.SemaphoreType.DMA((2,)), pltpu.SemaphoreType.DMA((2,))]
        aliases[8] = 1
    return pl.pallas_call(
        functools.partial(step_kernel, chunk, relay),
        out_shape=out_shape,
        in_specs=[SMEM, SMEM, SMEM, ANY, ANY, ANY, ANY, acc_spec, ANY],
        out_specs=out_specs,
        scratch_shapes=scratch,
        input_output_aliases=aliases,
        compiler_params=pltpu.CompilerParams(vmem_limit_bytes=48 << 20),
        cost_estimate=pl.CostEstimate(flops=4 * chunk * side * side * columns, bytes_accessed=2 * chunk * side * (4 * side + 4 * columns), transcendentals=0),
        name="step" if relay else "last",
    )(where, sched, t.reshape(1), ra, rb, tiles, panel, acc, log)


def blank(shape, dtype):
    return pl.pallas_call(lambda out: None, out_shape=jax.ShapeDtypeStruct(shape, dtype), out_specs=ANY, name="blank")()


def scatter_sum(total, n_col, n_layer):
    columns = total.shape[1]
    parts = total.reshape(n_col, n_layer, -1, columns)
    mine = lax.axis_index("layer")
    kept = lax.dynamic_index_in_dim(parts, mine, 1, keepdims=False)
    for k in range(1, n_layer):
        away = lax.dynamic_index_in_dim(parts, (mine + k) % n_layer, 1, keepdims=False)
        kept = kept + lax.ppermute(away, "layer", [(i, (i + k) % n_layer) for i in range(n_layer)])
    mine = lax.axis_index("col")
    result = lax.dynamic_index_in_dim(kept, mine, 0, keepdims=False)
    kept = kept.astype(jnp.bfloat16)
    for k in range(1, n_col):
        away = lax.dynamic_index_in_dim(kept, (mine + k) % n_col, 0, keepdims=False)
        result = result + lax.ppermute(away, "col", [(i, (i + k) % n_col) for i in range(n_col)]).astype(jnp.float32)
    return result


def local(n_row, n_col, n_layer, occupancy, tiles, panel):
    tile_rows, width = occupancy.shape
    slots, side = tiles.shape[2], tiles.shape[3]
    tiles = tiles.reshape(slots, side, side)
    panel = panel.reshape(width, side, -1)
    order = ring_order(n_row)
    up = [(order[p], order[(p + 1) % n_row]) for p in range(n_row)]
    down = [(b, a) for a, b in up]

    def gather_product(chunk):
        most = -(-slots // (2 * chunk))
        steps = (n_row - 2) * max(most, LATENCY) + most + 4
        first = [tiles[k * chunk:(k + 1) * chunk] for k in range(4) if (k + 1) * chunk <= slots]
        first = first + first[: 4 - len(first)]
        ra = lax.ppermute(first[0], "row", up)
        rb = lax.ppermute(first[1], "row", down)
        where, sched, meta = plan(occupancy, order, slots, chunk, steps)
        acc = own_product(where, meta, tiles, panel, tile_rows)
        log = blank((2, steps, chunk, side, side), tiles.dtype)

        def advance(t, sa, sb, ra, rb, acc, log):
            na = lax.ppermute(sa, "row", up)
            nb = lax.ppermute(sb, "row", down)
            acc, log, sa, sb = step(where, sched, t, ra, rb, tiles, panel, acc, log)
            return sa, sb, na, nb, acc, log

        state = advance(jnp.int32(1), first[2], first[3], ra, rb, acc, log)

        def body(carry):
            t, state = carry
            for u in range(2):
                state = advance(t + u, *state)
            return t + 2, state

        t, (_, _, ra, rb, acc, log) = lax.while_loop(lambda c: c[0] < meta[0], body, (jnp.int32(2), state))
        (acc,) = step(where, sched, t, ra, rb, tiles, panel, acc, log, relay=False)
        return acc

    coarse, fine = max(1, slots // 8), max(1, slots // 16)
    if coarse == fine:
        acc = gather_product(coarse)
    else:
        many = jnp.sum(occupancy) > (n_row - 1) * slots
        acc = lax.cond(many, lambda: gather_product(coarse), lambda: gather_product(fine))
    return scatter_sum(acc, n_col, n_layer)


def solution(mesh):
    placed = (
        P(None, ("col", "layer")),
        P(("col", "layer"), "row", None, None, None),
        P(("col", "layer"), "row"),
    )
    sizes = tuple(mesh.shape[name] for name in ("row", "col", "layer"))
    return jax.shard_map(
        functools.partial(local, *sizes), mesh=mesh, in_specs=placed, out_specs=P(("col", "layer"), "row"), check_vma=False
    )
```
